128 devices in a mesh: freq: 8 (over x, z_hi), param: 16 (over y, z_lo, core).
Axes of the slice: x: 4, y: 4, z: 4 (z_hi: 2, z_lo: 2; z = z_hi * 2 + z_lo), core: 2. Of those that a mesh axis runs over, the one named last changes fastest.
Arguments:
- sources: float32 [4, 420, 2048], P(None, None, ('param', 'freq')), may hold values from -6 to 6
- kernel: bfloat16 [424, 2, 600, 2048], P('freq', None, None, 'param'), may hold values from -0.09375 to 0.09375
- bin_of_slot: int32 [424], replicated, may hold values from 0 to 420, as said below
Outputs:
- observations: float32 [4, 420, 600], P(None, None, 'freq')
The draws below stay inside these ranges and needn't reach their ends.
Inputs may be any that keep to these rules, and one draw needn't show every extreme that they name: `bin_of_slot`: every bin from 0 to 420 is named by at least one slot; the other slots name bins again.
All inputs are finite; a program needn't handle non-finite values.
Results may differ from the reference program's by a relative error of at most 0.0031.
Values may be sent and summed in bfloat16 or wider, within the bound.
A program may use at most 64 MiB of HBM per device.

```python
import math
import jax
import jax.numpy as jnp
from jax import lax

NT = 420
NS = 600
SCEN = 4
NFB = 421
SLOTS = 424
NM = 2048


def draw_bin_of_slot(key, part):
    base_key = jax.random.fold_in(key, 7)
    first_key, second_key = jax.random.split(base_key)
    extra = jax.random.randint(first_key, (SLOTS - NFB,), 0, NFB, dtype=jnp.int32)
    listed = jnp.concatenate([jnp.arange(NFB, dtype=jnp.int32), extra])
    order = jax.random.permutation(second_key, SLOTS)
    return listed[order].astype(jnp.int32)


def level_of(stream_key, dims, cuts, least, largest):
    loudness = 1.0
    for axis_at, shards_of in cuts:
        draws = jax.random.uniform(jax.random.fold_in(jax.random.fold_in(stream_key, 6), axis_at), (shards_of,), jnp.float32, least / len(cuts), largest / len(cuts))
        loudness = loudness * jnp.repeat(jnp.exp(draws), dims[axis_at] // shards_of).reshape((-1,) + (1,) * (len(dims) - 1 - axis_at))
    return loudness


def noise(own_key, dims, width, most, cuts=(), held_as=jnp.bfloat16):
    factor_of = level_of(own_key, dims, cuts, -0.22, 0.18) if cuts else 1.0
    drawn = jax.random.normal(own_key, dims, jnp.float32) * width * factor_of
    return jnp.minimum(jnp.maximum(drawn, -most), most).astype(held_as)


def setup_inputs(seed: int = 0) -> dict:
    key_list = jax.random.split(jax.random.key(seed), 4)
    return {
        "sources": noise(key_list[0], (SCEN, NT, NM), 1.0, 6.0, ((2, 128),), jnp.float32),
        "kernel": noise(key_list[1], (SLOTS, 2, NS, NM), (2 * NM) ** -0.5, 0.09375, ((0, 8), (3, 16))),
        "bin_of_slot": draw_bin_of_slot(jax.random.fold_in(key_list[3], 71), 0),
    }


def angle_tables(bins, steps, scale):
    times = jnp.arange(steps, dtype=jnp.int32)
    phase = bins[:, None].astype(jnp.int32) * times[None, :] % (2 * steps)
    angle = phase.astype(jnp.float32) * (2.0 * math.pi / (2 * steps))
    return (jnp.cos(angle) * scale, jnp.sin(angle) * scale)

def reference(sources, kernel, bin_of_slot):
    highest = lax.Precision.HIGHEST
    cos_fwd, sin_fwd = angle_tables(bin_of_slot, NT, 1.0 / math.sqrt(NT))
    spec_real = jnp.einsum('st,ctj->scj', cos_fwd, sources, precision=highest).astype(jnp.bfloat16)
    spec_imag = jnp.einsum('st,ctj->scj', -sin_fwd, sources, precision=highest).astype(jnp.bfloat16)

    def respond(items):
        block, real_part, imag_part = items
        real = jnp.dot(real_part, block[0].T, preferred_element_type=jnp.float32) - jnp.dot(imag_part, block[1].T, preferred_element_type=jnp.float32)
        imag = jnp.dot(imag_part, block[0].T, preferred_element_type=jnp.float32) + jnp.dot(real_part, block[1].T, preferred_element_type=jnp.float32)
        return (real, imag)
    resp_real, resp_imag = lax.map(respond, (kernel, spec_real, spec_imag))
    weights = jnp.where((bin_of_slot == 0) | (bin_of_slot == NT), jnp.float32(1.0), jnp.float32(2.0))
    cos_inv, sin_inv = angle_tables(bin_of_slot, NT, 1.0 / math.sqrt(2.0 * (NT + 1)))
    cos_inv = cos_inv * weights[:, None]
    sin_inv = sin_inv * weights[:, None]
    observations = jnp.einsum('st,sck->ctk', cos_inv, resp_real, precision=highest) - jnp.einsum('st,sck->ctk', sin_inv, resp_imag, precision=highest)
    return observations
```

```python
import functools
import math

import jax
import jax.numpy as jnp
from jax import lax
from jax.experimental import pallas as pl
from jax.experimental.pallas import tpu as pltpu
from jax.sharding import PartitionSpec as P

MESH = pl.DeviceIdType.MESH
F = 8
PN = 16
SL = 53
NG = 4
NT = 420
NTP = 512
NS = 600
ROWS = 40
KD = 5
NMSG = 15
BF = jnp.bfloat16
F32 = jnp.float32
NT_DIMS = (((1,), (1,)), ((), ()))


def sincos(v):
    x = v - 840.0 * jnp.floor(v * (1.0 / 840.0) + 0.5)
    h = x * (math.pi / 840.0)
    z = h * h
    s = jnp.full_like(z, 1.0 / math.factorial(13))
    sign = -1.0
    for n in (11, 9, 7, 5, 3, 1):
        s = s * z + sign / math.factorial(n)
        sign = -sign
    s = s * h
    c = jnp.full_like(z, 1.0 / math.factorial(12))
    sign = -1.0
    for n in (10, 8, 6, 4, 2, 0):
        c = c * z + sign / math.factorial(n)
        sign = -sign
    return 1.0 - 2.0 * (s * s), 2.0 * (s * c)


def split(x):
    hi = x.astype(BF)
    lo = (x - hi.astype(F32)).astype(BF)
    return hi, lo


def body(
    src, bins, kern, out,
    kv, thi, tlo, s2, b8, spec, ra, wf, stage, xr, zs, zr, ob, og,
    ksem, fs, fr, ps, pr, zss, zrs, osem, ors, lsem,
):
    f = lax.axis_index("freq")
    p = lax.axis_index("param")
    gid = p * F + f
    home = gid // NMSG
    piece = gid % NMSG

    for g in range(NG):
        n = min(16, SL - 16 * g)
        pltpu.make_async_copy(
            kern.at[pl.ds(16 * g, n)], kv.at[pl.ds(16 * g, n)], ksem.at[g]
        ).start()

    barrier = pltpu.get_barrier_semaphore()

    def greet(df, dp):
        pl.semaphore_signal(barrier, inc=1, device_id=(df, dp), device_id_type=MESH)

    def greet_freq(d, _):
        greet(lax.rem(f + d, F), p)
        return 0

    def greet_param(d, _):
        greet(f, lax.rem(p + d, PN))
        return 0

    def greet_piece(m, _):
        other = f * NMSG + m

        @pl.when(other != gid)
        def _():
            greet(lax.rem(other, F), other // F)

        return 0

    lax.fori_loop(1, F, greet_freq, 0)
    lax.fori_loop(1, PN, greet_param, 0)
    lax.fori_loop(0, NMSG, greet_piece, 0)

    s2[:, 384:512] = jnp.zeros((128, 128), BF)
    hi, lo = split(src[...])
    s2[0:64, 0:NT] = hi
    s2[64:128, 0:NT] = lo

    b8[...] = jnp.zeros((128, 128), F32)
    for i in range(F):
        b8[i : i + 1, 0:SL] = bins[0:1, SL * i : SL * (i + 1)].astype(F32)
    bv = b8[0:8, :]
    c8, s8 = sincos(bv * 128.0)
    b8[8:16, :] = c8
    b8[16:24, :] = s8
    cols = b8[...].T
    w8 = jnp.where((bv == 0.0) | (bv == float(NT)), 1.0, 2.0)
    er = lax.broadcasted_iota(jnp.int32, (128, 128), 0)
    ec = lax.broadcasted_iota(jnp.int32, (128, 128), 1)
    spread = (er == (ec // 32) * 16 + ec % 16).astype(F32).astype(BF)
    w8 = jnp.dot(w8.astype(BF), spread, preferred_element_type=F32) * (1.0 / math.sqrt(NT))

    ramp = lax.broadcasted_iota(jnp.int32, (64, 128), 1).astype(F32)
    for i in range(F):
        bc = jnp.broadcast_to(cols[0:64, i : i + 1], (64, 128))
        cs = jnp.broadcast_to(cols[0:64, 8 + i : 9 + i], (64, 128))
        sn = jnp.broadcast_to(cols[0:64, 16 + i : 17 + i], (64, 128))
        c, s = sincos(bc * ramp)
        for a in range(4):
            if a:
                c, s = c * cs - s * sn, s * cs + c * sn
            at = slice(128 * a, 128 * (a + 1))
            chi, clo = split(c.reshape(4, 16, 128))
            shi, slo = split((-s).reshape(4, 16, 128))
            thi[i, :, 0, :, at] = chi
            thi[i, :, 1, :, at] = shi
            tlo[i, :, 0, :, at] = clo
            tlo[i, :, 1, :, at] = slo
        th = thi[i].reshape(128, NTP)
        tl = tlo[i].reshape(128, NTP)
        both = lax.dot_general(s2[...], th, NT_DIMS, preferred_element_type=F32)
        low = lax.dot_general(s2[0:64, :], tl, NT_DIMS, preferred_element_type=F32)
        a_i = (both[0:64] + both[64:128] + low) * w8[i : i + 1, :]
        spec[i] = a_i.astype(BF)
        if i == 0:
            extra = jnp.where(gid < F * NMSG, PN - (home == f).astype(jnp.int32), 0)
            pl.semaphore_wait(barrier, F - 1 + PN - 1 + extra)

        @pl.when(f != i)
        def _():
            pltpu.make_async_remote_copy(
                src_ref=spec.at[i], dst_ref=ra.at[f], send_sem=fs.at[i], recv_sem=fr.at[f],
                device_id=(i, p), device_id_type=MESH,
            ).start()

        @pl.when(f == i)
        def _():
            pltpu.make_async_copy(spec.at[i], ra.at[f], fr.at[f]).start()

    qr = lax.broadcasted_iota(jnp.int32, (192, 640), 0)
    qc = lax.broadcasted_iota(jnp.int32, (192, 640), 1)
    r24 = qr % 24
    want = (qr // 24) * KD + r24 // 4
    q = jnp.where((qc % ROWS == want) & (r24 < 4 * KD), 1.0, 0.0).astype(BF)

    for i in range(F):
        pltpu.make_async_copy(spec.at[i], ra.at[i], fr.at[i]).wait()

    lane = lax.broadcasted_iota(jnp.int32, (128, 128), 1)
    chunk = lane // 32
    part = (lane // 16) % 2
    amp = [ra[:, 16 * c : 16 * (c + 1), :].reshape(128, 128).astype(F32) for c in range(4)]
    for g in range(NG):
        w0 = jnp.zeros((128, 128), F32)
        for c in range(4):
            shift = (32 * (c - g)) % 128
            moved = pltpu.roll(amp[c], shift, 1) if shift else amp[c]
            w0 = jnp.where(chunk == c, moved, w0)
        w1 = jnp.where(part == 0, -pltpu.roll(w0, 112, 1), pltpu.roll(w0, 16, 1))
        wf[g, 0:128, :] = w0.astype(BF)
        wf[g, 128:256, :] = w1.astype(BF)

    lane16 = lax.broadcasted_iota(jnp.int32, (256, 128), 1) % 16
    for g in range(NG):
        n = min(16, SL - 16 * g)
        pltpu.make_async_copy(
            kern.at[pl.ds(16 * g, n)], kv.at[pl.ds(16 * g, n)], ksem.at[g]
        ).wait()
        acc = None
        wg = wf[g]
        for i in range(n):
            s = 16 * g + i
            ws = jnp.where(lane16 == i, wg, jnp.zeros_like(wg))
            lhs = jnp.concatenate([kv[s, 0], kv[s, 1]], axis=1)
            term = jnp.dot(lhs, ws, preferred_element_type=F32)
            acc = term if acc is None else acc + term
        stage[g] = acc.astype(BF)

        def send(d, _):
            to = lax.rem(p + d, PN)

            @pl.when(to < NMSG)
            def _():
                rows = pl.ds(pl.multiple_of(to * ROWS, 8), ROWS)
                mine = pl.ds(pl.multiple_of(p * ROWS, 8), ROWS)
                pltpu.make_async_remote_copy(
                    src_ref=stage.at[g, rows], dst_ref=xr.at[g, mine],
                    send_sem=ps.at[g, to], recv_sem=pr.at[g, p],
                    device_id=(f, to), device_id_type=MESH,
                ).start()

            return 0

        lax.fori_loop(1, PN, send, 0)

        @pl.when(p < NMSG)
        def _():
            mine = pl.ds(pl.multiple_of(p * ROWS, 8), ROWS)
            pltpu.make_async_copy(stage.at[g, mine], xr.at[g, mine], pr.at[g, p]).start()

    @pl.when(p < NMSG)
    def _():
        def arrive(j, _):
            rows = pl.ds(pl.multiple_of(j * ROWS, 8), ROWS)
            for g in range(NG):
                pltpu.make_async_copy(xr.at[g, rows], xr.at[g, rows], pr.at[g, j]).wait()
            return 0

        lax.fori_loop(0, PN, arrive, 0)
        lanes = lax.broadcasted_iota(jnp.int32, (192, 128), 1) // 32
        scen = lax.broadcasted_iota(jnp.int32, (192, 128), 0) % 4
        y = [jnp.dot(q, xr[g], preferred_element_type=F32) for g in range(NG)]
        zsum = jnp.zeros((192, 128), F32)
        for d in range(4):
            u = y[d]
            for c in range(1, 4):
                u = jnp.where(scen == c, y[(c + d) % 4], u)
            if d:
                u = pltpu.roll(u, 32 * d, 1)
            zsum = jnp.where(lanes == (scen + d) % 4, u, zsum)
        zs[...] = zsum.reshape(F, 24, 128)

        def swap(d, _):
            to = lax.rem(f + d, F)
            pltpu.make_async_remote_copy(
                src_ref=zs.at[to], dst_ref=zr.at[f], send_sem=zss.at[to], recv_sem=zrs.at[f],
                device_id=(to, p), device_id_type=MESH,
            ).start()
            return 0

        lax.fori_loop(1, F, swap, 0)
        pltpu.make_async_copy(zs.at[f], zr.at[f], zrs.at[f]).start()

        def swapped(j, _):
            pltpu.make_async_copy(zs.at[j], zr.at[j], zrs.at[j]).wait()
            return 0

        lax.fori_loop(0, F, swapped, 0)

        r = jnp.concatenate([zr[i] for i in range(F)], axis=1)
        rhi, rlo = split(r)
        th = thi[...].reshape(1024, NTP)
        tl = tlo[...].reshape(1024, NTP)
        o = jnp.dot(rhi, th, preferred_element_type=F32)
        o = o + jnp.dot(rlo, th, preferred_element_type=F32)
        o = o + jnp.dot(rhi, tl, preferred_element_type=F32)
        ob[...] = (o * (1.0 / math.sqrt(2.0 * (NT + 1)))).astype(BF)

        def spread_out(d, _):
            to = lax.rem(p + d, PN)
            here = (home == f) & (d == 0)

            @pl.when(jnp.logical_not(here))
            def _():
                pltpu.make_async_remote_copy(
                    src_ref=ob, dst_ref=og.at[piece], send_sem=osem.at[to], recv_sem=ors.at[piece],
                    device_id=(home, to), device_id_type=MESH,
                ).start()

            @pl.when(here)
            def _():
                pltpu.make_async_copy(ob, og.at[piece], ors.at[piece]).start()

            return 0

        lax.fori_loop(0, PN, spread_out, 0)

    def landed(m, _):
        pltpu.make_async_copy(ob, og.at[m], ors.at[m]).wait()
        return 0

    lax.fori_loop(0, NMSG, landed, 0)
    for m in range(NMSG):
        out[m] = og[m, 0:20, 0:NT].astype(F32)

    for i in range(F):

        @pl.when(f != i)
        def _():
            pltpu.make_async_copy(spec.at[i], spec.at[i], fs.at[i]).wait()

    def sent(d, _):
        to = lax.rem(p + d, PN)

        @pl.when(to < NMSG)
        def _():
            rows = pl.ds(pl.multiple_of(to * ROWS, 8), ROWS)
            for g in range(NG):
                pltpu.make_async_copy(stage.at[g, rows], stage.at[g, rows], ps.at[g, to]).wait()

        return 0

    lax.fori_loop(1, PN, sent, 0)

    @pl.when(p < NMSG)
    def _():
        def swap_sent(d, _):
            to = lax.rem(f + d, F)
            pltpu.make_async_copy(zs.at[to], zs.at[to], zss.at[to]).wait()
            return 0

        lax.fori_loop(1, F, swap_sent, 0)

        def spread_sent(d, _):
            to = lax.rem(p + d, PN)

            @pl.when(jnp.logical_not((home == f) & (d == 0)))
            def _():
                pltpu.make_async_copy(ob, ob, osem.at[to]).wait()

            return 0

        lax.fori_loop(0, PN, spread_sent, 0)


def shards(sources, kernel, bin_of_slot):
    src = jnp.transpose(sources, (0, 2, 1)).reshape(64, NT)
    bins = bin_of_slot.reshape(1, F * SL)
    dma = pltpu.SemaphoreType.DMA
    o = pl.pallas_call(
        body,
        out_shape=jax.ShapeDtypeStruct((NMSG, 20, NT), F32),
        in_specs=[
            pl.BlockSpec(memory_space=pltpu.VMEM),
            pl.BlockSpec(memory_space=pltpu.VMEM),
            pl.BlockSpec(memory_space=pl.ANY),
        ],
        out_specs=pl.BlockSpec(memory_space=pltpu.VMEM),
        scratch_shapes=[
            pltpu.VMEM((SL, 2, NS, 128), BF),
            pltpu.VMEM((F, NG, 2, 16, NTP), BF),
            pltpu.VMEM((F, NG, 2, 16, NTP), BF),
            pltpu.VMEM((128, NTP), BF),
            pltpu.VMEM((128, 128), F32),
            pltpu.VMEM((F, 64, 128), BF),
            pltpu.VMEM((F, 64, 128), BF),
            pltpu.VMEM((NG, 256, 128), BF),
            pltpu.VMEM((NG, NS, 128), BF),
            pltpu.VMEM((NG, PN * ROWS, 128), BF),
            pltpu.VMEM((F, 24, 128), F32),
            pltpu.VMEM((F, 24, 128), F32),
            pltpu.VMEM((24, NTP), BF),
            pltpu.VMEM((NMSG, 24, NTP), BF),
            dma((NG,)),
            dma((F,)),
            dma((F,)),
            dma((NG, PN)),
            dma((NG, PN)),
            dma((F,)),
            dma((F,)),
            dma((PN,)),
            dma((NMSG,)),
            dma((1,)),
        ],
        compiler_params=pltpu.CompilerParams(
            collective_id=0, has_side_effects=True, vmem_limit_bytes=60 * 1024 * 1024
        ),
    )(src, bins, kernel)
    return jnp.transpose(o.reshape(75, 4, NT), (1, 2, 0))


def solution(mesh):
    return jax.shard_map(
        shards,
        mesh=mesh,
        in_specs=(P(None, None, ("param", "freq")), P("freq", None, None, "param"), P()),
        out_specs=P(None, None, "freq"),
        check_vma=False,
    )
```
